256 devices in a mesh: seq: 32 (over z, y), head: 8 (over x, core).
Axes of the slice: x: 4, y: 4, z: 8, core: 2. Of those that a mesh axis runs over, the one named last changes fastest.
Arguments:
- queries: bfloat16 [65536, 4096], P('seq', 'head'), may hold values from -6 to 6
- key_inputs: bfloat16 [65536, 4096], P('seq', 'head'), may hold values from -6 to 6
- values: bfloat16 [65536, 4096], P('seq', 'head'), may hold values from -36 to 36
- out_gain: float32 [4096], replicated, may hold values from 0.25 to 1.75
Outputs:
- normed: bfloat16 [65536, 4096], P(('seq', 'head'))
The draws below stay inside these ranges and needn't reach their ends.
All inputs are finite; a program needn't handle non-finite values.
Results may differ from the reference program's by a relative error of at most 0.0056.
Values may be sent and summed in bfloat16 or wider, within the bound.
No kernel may reach another device: no remote copies, remote signals or barrier semaphores. Data moves between devices by JAX's collectives and lax.ppermute only.
A program may use at most 64 MiB of HBM per device.

```python
import math
import jax
import jax.numpy as jnp
from jax import lax

HEADS = 32
HD = 128
BLOCK = 512
TOKENS = 65536


def draw_values(key, part):
    key_rows, key_cols, key_noise = jax.random.split(key, 3)
    features = HEADS * HD
    row_scale = jnp.exp(jax.random.uniform(key_rows, (TOKENS, 1), jnp.float32, math.log(0.3), math.log(3.0)))
    col_scale = jnp.exp(jax.random.uniform(key_cols, (1, features), jnp.float32, math.log(0.3), math.log(3.0)))
    base = jnp.clip(jax.random.normal(key_noise, (TOKENS, features), jnp.float32), -4.0, 4.0)
    return (row_scale * col_scale * base).astype(jnp.bfloat16)


def level_of(key, shape, shards, smallest, top_value):
    loudness = 1.0
    for dim, shards_of in shards:
        steps = jax.random.uniform(jax.random.fold_in(jax.random.fold_in(key, 6), dim), (shards_of,), jnp.float32, smallest / len(shards), top_value / len(shards))
        loudness = loudness * jnp.repeat(jnp.exp(steps), shape[dim] // shards_of).reshape((-1,) + (1,) * (len(shape) - 1 - dim))
    return loudness


def bell_draw(own_key, extent, width, limit, pieces=(), held_as=jnp.bfloat16):
    array = jax.random.normal(own_key, extent, jnp.float32) * width
    if len(pieces) > 0:
        array = level_of(own_key, extent, pieces, -0.22, 0.18) * array
    return jnp.clip(array, min=-limit, max=limit).astype(held_as)


def setup_inputs(seed: int = 0) -> dict:
    key_list = jax.random.split(jax.random.key(seed), 5)
    queries = bell_draw(key_list[0], (TOKENS, HEADS * HD), 1.0, 6.0, ((0, 32), (1, 8)))
    key_inputs = bell_draw(key_list[1], (TOKENS, HEADS * HD), 1.0, 6.0, ((0, 32), (1, 8)))
    values = draw_values(jax.random.fold_in(key_list[4], 71), 0)
    out_gain = jnp.clip(1.0 + 0.15 * jax.random.normal(key_list[3], (HEADS * HD,), jnp.float32), 0.25, 1.75)
    return dict(queries=queries, key_inputs=key_inputs, values=values, out_gain=out_gain)


def reference(queries, key_inputs, values, out_gain):
    token_count = queries.shape[0]
    block_count = token_count // BLOCK
    query_map = jax.nn.silu(queries.astype(jnp.float32)).astype(jnp.bfloat16)
    key_map = jax.nn.silu(key_inputs.astype(jnp.float32)).astype(jnp.bfloat16)
    causal = jnp.tril(jnp.ones((BLOCK, BLOCK), dtype=bool))

    def head_fn(head_index):
        first = (head_index * HD).astype(jnp.int32)
        head_queries = lax.dynamic_slice_in_dim(query_map, first, HD, 1).reshape(block_count, BLOCK, HD)
        head_keys = lax.dynamic_slice_in_dim(key_map, first, HD, 1).reshape(block_count, BLOCK, HD)
        head_values = lax.dynamic_slice_in_dim(values, first, HD, 1).reshape(block_count, BLOCK, HD)

        def advance(carry_state, blocks):
            block_queries, block_keys, block_values = blocks
            scores = jnp.dot(block_queries, block_keys.T, preferred_element_type=jnp.float32)
            scores = jnp.where(causal, scores, 0.0).astype(jnp.bfloat16)
            inside = jnp.dot(scores, block_values, preferred_element_type=jnp.float32)
            carried = jnp.dot(block_queries.astype(jnp.float32), carry_state, precision=lax.Precision.HIGHEST)
            carry_state = carry_state + jnp.dot(block_keys.T, block_values, preferred_element_type=jnp.float32)
            return (carry_state, (inside + carried).astype(jnp.bfloat16))
        _, head_outputs = lax.scan(advance, jnp.zeros((HD, HD), jnp.float32), (head_queries, head_keys, head_values))
        return head_outputs.reshape(token_count, HD)
    all_heads = lax.map(head_fn, jnp.arange(HEADS, dtype=jnp.int32))
    attended = jnp.transpose(all_heads, (1, 0, 2)).reshape(token_count, HEADS * HD)
    wide_out = attended.astype(jnp.float32)
    mean_square = lax.optimization_barrier(jnp.mean(wide_out * wide_out, axis=1, keepdims=True))
    return (wide_out * lax.rsqrt(mean_square + 1e-06) * out_gain.astype(jnp.float32)).astype(jnp.bfloat16)
```

```python
import jax
import jax.numpy as jnp
from jax import lax
from jax.experimental import pallas as pl
from jax.experimental.pallas import tpu as pltpu
from jax.sharding import PartitionSpec as P

HD = 128
BLOCK = 512
F32 = jnp.float32
BF16 = jnp.bfloat16
WHOLE = pl.BlockSpec(memory_space=pltpu.VMEM)
SCALAR = pl.BlockSpec(memory_space=pltpu.SMEM)
PARAMS = pltpu.CompilerParams(vmem_limit_bytes=24 * 1024 * 1024)


def near(x):
    return pltpu.with_memory_space_constraint(x, pltpu.VMEM)


def far(x):
    return pltpu.with_memory_space_constraint(x, pltpu.HBM)


def silu(u):
    half = 0.5 * u.astype(F32)
    return (half + half * jnp.tanh(half)).astype(BF16)


def state_kernel(k_ref, v_ref, local_ref, total_ref):
    b = pl.program_id(0)

    @pl.when(b == 0)
    def _():
        total_ref[...] = jnp.zeros_like(total_ref)

    local_ref[0] = total_ref[...]
    for h in range(total_ref.shape[0]):
        cols = slice(h * HD, (h + 1) * HD)
        key_map = silu(k_ref[:, cols])
        total_ref[h] += lax.dot_general(
            key_map, v_ref[:, cols], (((0,), (0,)), ((), ())), preferred_element_type=F32
        )


def shard_states(k, v):
    rows, feats = k.shape
    heads = feats // HD
    blocks = rows // BLOCK
    spec = pl.BlockSpec((BLOCK, feats), lambda b: (b, 0))
    return pl.pallas_call(
        state_kernel,
        grid=(blocks,),
        in_specs=[spec, spec],
        out_specs=[
            pl.BlockSpec((1, heads, HD, HD), lambda b: (b, 0, 0, 0)),
            pl.BlockSpec((heads, HD, HD), lambda b: (0, 0, 0)),
        ],
        out_shape=[pltpu.HBM((blocks, heads, HD, HD), F32), pltpu.HBM((heads, HD, HD), F32)],
        compiler_params=PARAMS,
        name="states",
    )(far(k), far(v))


def inside_kernel(q_ref, k_ref, v_ref, out_ref, qm_ref):
    half = BLOCK // 2
    row = lax.broadcasted_iota(jnp.int32, (half, half), 0)
    col = lax.broadcasted_iota(jnp.int32, (half, half), 1)
    causal = row >= col
    nt = (((1,), (1,)), ((), ()))
    for h in range(q_ref.shape[1] // HD):
        cols = slice(h * HD, (h + 1) * HD)
        qm = silu(q_ref[:, cols])
        km = silu(k_ref[:, cols])
        vv = v_ref[:, cols]
        qm_ref[:, cols] = qm
        for t in range(2):
            rows = slice(t * half, (t + 1) * half)
            diag = lax.dot_general(qm[rows], km[rows], nt, preferred_element_type=F32)
            diag = jnp.where(causal, diag, 0.0).astype(BF16)
            acc = jnp.dot(diag, vv[rows], preferred_element_type=F32)
            if t == 1:
                past = lax.dot_general(qm[rows], km[:half], nt, preferred_element_type=F32).astype(BF16)
                acc = acc + jnp.dot(past, vv[:half], preferred_element_type=F32)
            out_ref[rows, cols] = acc


def inside_part(q, k, v, part, parts):
    rows, feats = q.shape
    feats = feats // parts
    blocks = rows // BLOCK
    spec = pl.BlockSpec((BLOCK, feats), lambda b: (b, part))
    return pl.pallas_call(
        inside_kernel,
        grid=(blocks,),
        in_specs=[spec, spec, spec],
        out_specs=[pl.BlockSpec((BLOCK, feats), lambda b: (b, 0))] * 2,
        out_shape=[pltpu.HBM((rows, feats), F32), pltpu.HBM((rows, feats), BF16)],
        compiler_params=PARAMS,
        name="inside",
    )(far(q), far(k), far(v))


def scan_kernel(x_ref, o_ref):
    run = jnp.zeros(x_ref.shape[1:], F32)
    for s in range(x_ref.shape[0]):
        o_ref[s] = run
        run = run + x_ref[s]


def scan_slices(x):
    return pl.pallas_call(
        scan_kernel,
        in_specs=[WHOLE],
        out_specs=pl.BlockSpec(x.shape, lambda: (0, 0, 0)),
        out_shape=pltpu.HBM(x.shape, F32),
        compiler_params=PARAMS,
        name="scan",
    )(near(x))


def carried_kernel(shifts, size, parts, me_ref, *refs):
    inside_refs, qm_refs = refs[:parts], refs[parts : 2 * parts]
    local_ref, prefix_ref = refs[2 * parts : 2 * parts + 2]
    out_refs = refs[2 * parts + 2 : -4]
    inside_buf, qm_buf, local_buf, sems = refs[-4:]
    count = out_refs[0].shape[0]
    per_part = prefix_ref.shape[0] // parts

    def copies(i):
        dest = lax.rem(me_ref[0] + shifts[i], size)
        rows = pl.ds(pl.multiple_of(dest * count, count), count)
        moves = [(local_ref.at[dest * count // BLOCK], local_buf.at[i])]
        for p in range(parts):
            moves.append((inside_refs[p].at[rows], inside_buf.at[i, p]))
            moves.append((qm_refs[p].at[rows], qm_buf.at[i, p]))
        return [pltpu.make_async_copy(a, b, sems.at[i, n]) for n, (a, b) in enumerate(moves)]

    for i in range(len(shifts)):
        for move in copies(i):
            move.start()
    for i, out_ref in enumerate(out_refs):
        for move in copies(i):
            move.wait()
        for h in range(prefix_ref.shape[0]):
            part, at = divmod(h, per_part)
            cols = slice(at * HD, (at + 1) * HD)
            state = local_buf[i, h] + prefix_ref[h]
            acc = inside_buf[i, part, :, cols]
            qm = qm_buf[i, part, :, cols]
            for _ in range(3):
                piece = state.astype(BF16)
                state = state - piece.astype(F32)
                acc = acc + jnp.dot(qm, piece, preferred_element_type=F32)
            out_ref[:, h * HD : (h + 1) * HD] = acc.astype(BF16)


def carried_rows(shifts, size, me, inside, qm, local, prefix):
    parts = len(inside)
    count = inside[0].shape[0] // size
    width = inside[0].shape[1]
    n = len(shifts)

    def kernel(*refs):
        carried_kernel(shifts, size, parts, *refs)

    return pl.pallas_call(
        kernel,
        in_specs=[SCALAR] + [pl.BlockSpec(memory_space=pl.ANY)] * (2 * parts + 1) + [WHOLE],
        out_specs=[WHOLE] * n,
        out_shape=[pltpu.VMEM((count, width * parts), BF16)] * n,
        scratch_shapes=[
            pltpu.VMEM((n, parts, count, width), F32),
            pltpu.VMEM((n, parts, count, width), BF16),
            pltpu.VMEM((n,) + local.shape[1:], F32),
            pltpu.SemaphoreType.DMA((n, 2 * parts + 1)),
        ],
        compiler_params=PARAMS,
        name="carried",
    )(me, *[far(x) for x in (*inside, *qm, local)], near(prefix))


def norm_kernel(shifts, step, me_ref, gain_ref, *refs):
    parts, out_ref = refs[:-1], refs[-1]
    feats = parts[0].shape[1]
    size = len(shifts)
    rows = pl.ds(pl.program_id(0) * step, step)
    total = None
    for part in parts:
        wide = part[rows].astype(F32)
        total = wide * wide if total is None else total + wide * wide
    mean = jnp.sum(total, axis=1, keepdims=True) * (1.0 / out_ref.shape[1])
    scale = lax.rsqrt(mean + 1e-06)
    for shift, part in zip(shifts, parts):
        src = lax.rem(me_ref[0] + (size - shift), size)
        at = pl.ds(pl.multiple_of(src * feats, feats), feats)
        out_ref[:, at] = (part[rows].astype(F32) * scale * gain_ref[:, at]).astype(BF16)


def norm_rows(shifts, me, gain, parts):
    rows, feats = parts[0].shape
    n = len(parts)
    step = 64

    def kernel(*refs):
        norm_kernel(shifts, step, *refs)

    return pl.pallas_call(
        kernel,
        grid=(rows // step,),
        in_specs=[SCALAR] + [WHOLE] * (n + 1),
        out_specs=pl.BlockSpec((step, n * feats), lambda i: (i, 0)),
        out_shape=jax.ShapeDtypeStruct((rows, n * feats), BF16),
        compiler_params=PARAMS,
        name="norm",
    )(me, gain, *[near(p) for p in parts])


def shards(queries, key_inputs, values, out_gain, seq_size, head_size):
    _, feats = queries.shape
    heads = feats // HD
    me = lax.axis_index("head").astype(jnp.int32).reshape(1)
    local, total = shard_states(key_inputs, values)
    slices = total.reshape(seq_size, heads * HD // seq_size, HD)
    slices = lax.all_to_all(slices, "seq", 0, 0, tiled=True)
    inside_a, qm_a = inside_part(queries, key_inputs, values, 0, 2)
    before = scan_slices(slices)
    prefix = lax.all_to_all(before, "seq", 0, 0, tiled=True)
    inside_b, qm_b = inside_part(queries, key_inputs, values, 1, 2)
    prefix = prefix.reshape(heads, HD, HD)
    order = [d for k in range(head_size // 2, 0, -1) for d in dict.fromkeys((k, head_size - k))] + [0]
    groups = [order[:1], order[1:3], order[3:]]
    parts = []
    inside, qm = (inside_a, inside_b), (qm_a, qm_b)
    for shifts in groups:
        out = carried_rows(tuple(shifts), head_size, me, inside, qm, local, prefix)
        for d, rows_out in zip(shifts, out):
            if d:
                rows_out = lax.ppermute(rows_out, "head", [(i, (i + d) % head_size) for i in range(head_size)])
            parts.append(rows_out)
    return norm_rows(tuple(order), me, out_gain.reshape(1, -1), parts)


def solution(mesh):
    seq_size, head_size = mesh.shape["seq"], mesh.shape["head"]

    def run(queries, key_inputs, values, out_gain):
        return shards(queries, key_inputs, values, out_gain, seq_size, head_size)

    return jax.shard_map(
        run,
        mesh=mesh,
        in_specs=(P("seq", "head"), P("seq", "head"), P("seq", "head"), P()),
        out_specs=P(("seq", "head"), None),
        check_vma=False,
    )
```
